32 devices in a mesh: depth: 4 (over z), rows: 2 (over core), cols: 4 (over y, x).
Axes of the slice: x: 2, y: 2, z: 4, core: 2. Of those that a mesh axis runs over, the one named last changes fastest.
Arguments:
- lower_panels: bfloat16 [8, 4, 1536, 1024], P('depth', None, None, ('rows', 'cols')), may hold values from -0.23925781 to 0.23925781
- upper_panels: bfloat16 [8, 1024, 6144], P('depth', 'rows', 'cols'), may hold values from -0.23925781 to 0.23925781
- given_inverse: bfloat16 [8, 1024, 1024], P('depth', 'rows'), may hold values from -0.05625 to 2, as said below
- structure: int32 [8, 48], P('depth'), may hold values 0 or 1
- ancestor_entries: float32 [6144, 6144], P(('depth', 'rows'), 'cols'), may hold values from -0.6 to 19.2, as said below
Outputs:
- column_factor: float32 [6144, 512], P(('depth', 'rows'))
- trailing: float32 [6144, 6144], P(('depth', 'rows'), 'cols')
The draws below stay inside these ranges and needn't reach their ends.
Inputs may be any that keep to these rules, and one draw needn't show every extreme that they name: `given_inverse`: off-diagonal entries are small against the diagonal. `ancestor_entries`: diagonal entries lie between 12.8 and 19.2.
All inputs are finite; a program needn't handle non-finite values. No bound on the sum of `structure` on one device may be relied on, other than what follows from the above.
Results may differ from the reference program's by a relative error of at most 0.0003.
Values may be sent and summed in bfloat16 or wider, within the bound.
No kernel may reach another device: no remote copies, remote signals or barrier semaphores. Data moves between devices by JAX's collectives and lax.ppermute only.
A program may use at most 128 MiB of HBM per device.

```python
import jax
import jax.numpy as jnp
from jax import lax

NS = 1024
NA = 6144
PW = 512
BLOCK = 128
NEWTON = 2
NSUB = 8
SPAN = 1536
N_DEPTH = 4


def draw_given_inverse(key, part):
    key_diag = jax.random.fold_in(key, 11)
    key_noise = jax.random.fold_in(key, 12)
    diagonal = jnp.exp(jax.random.uniform(key_diag, (NSUB, NS), jnp.float32, jnp.log(0.5), jnp.log(2.0)))
    noise = jnp.clip(jax.random.normal(key_noise, (NSUB, NS, NS), jnp.float32), -6.0, 6.0)
    noise = noise * (0.3 / NS ** 0.5)
    identity = jnp.eye(NS, dtype=jnp.float32)
    return (noise * (1.0 - identity) + identity * diagonal[:, :, None]).astype(jnp.bfloat16)


def draw_ancestor_entries(key, part):
    key_jitter = jax.random.fold_in(key, 21)
    key_noise = jax.random.fold_in(key, 22)
    noise = jnp.clip(jax.random.normal(key_noise, (NA, NA), jnp.float32), -6.0, 6.0) * 0.1
    jitter = jax.random.uniform(key_jitter, (NA,), jnp.float32, -1.0, 1.0)
    identity = jnp.eye(NA, dtype=jnp.float32)
    return noise * (1.0 - identity) + identity * (16.0 * (1.0 + 0.2 * jitter))[:, None]


def set_ends(array, own_key, least, top_value):
    spot = [jax.random.randint(jax.random.fold_in(own_key, axis), (), 0, length) for axis, length in enumerate(array.shape)]
    main_axis = array.shape.index(max(array.shape))
    beside = spot[:main_axis] + [(spot[main_axis] + 1) % array.shape[main_axis]] + spot[main_axis + 1:]
    return array.at[tuple(spot)].set(least).at[tuple(beside)].set(top_value)


def level_of(own_key, shape, split, low, top_value):
    gain = 1.0
    for position, blocks in split:
        draws = jax.random.uniform(jax.random.fold_in(jax.random.fold_in(own_key, 6), position), (blocks,), jnp.float32, low / len(split), top_value / len(split))
        gain = gain * jnp.repeat(jnp.exp(draws), shape[position] // blocks).reshape((-1,) + (1,) * (len(shape) - 1 - position))
    return gain


def gaussian(stream_key, dims, scale, most, pieces=(), kind=jnp.bfloat16):
    level = level_of(stream_key, dims, pieces, -0.22, 0.18) if pieces else 1.0
    result = jax.random.normal(stream_key, dims, jnp.float32) * scale * level
    return jnp.minimum(jnp.maximum(result, -most), most).astype(kind)


def setup_inputs(seed: int = 0) -> dict:
    splits = jax.random.split(jax.random.key(seed), 6)
    return {
        "lower_panels": gaussian(splits[0], (NSUB, N_DEPTH, SPAN, NS), 0.04, 0.23925781, ((0, 4), (3, 8))),
        "upper_panels": gaussian(splits[1], (NSUB, NS, NA), 0.04, 0.23925781, ((0, 4), (1, 2), (2, 4))),
        "given_inverse": draw_given_inverse(jax.random.fold_in(splits[5], 71), 0),
        "structure": set_ends((jax.random.randint(splits[3], (NSUB, NA // BLOCK), 0, 4) < 3).astype(jnp.int32), jax.random.fold_in(splits[3], 1), 0, 1),
        "ancestor_entries": draw_ancestor_entries(jax.random.fold_in(splits[5], 71), 0),
    }


def reference(lower_panels, upper_panels, given_inverse, structure, ancestor_entries):
    highest = lax.Precision.HIGHEST
    kept_rows = jnp.repeat(structure.astype(jnp.float32), BLOCK, axis=1)
    lower_flat = lower_panels.reshape(NSUB, NA, NS)

    def add_subtree(running, members):
        lower_block, upper_block, inverse_block, kept_block = members
        lower_masked = lower_block.astype(jnp.float32) * kept_block[:, None]
        upper_masked = upper_block.astype(jnp.float32) * kept_block[None, :]
        applied = jnp.dot(inverse_block.astype(jnp.float32), upper_masked, precision=highest).astype(jnp.bfloat16)
        return running + jnp.dot(lower_masked, applied.astype(jnp.float32), precision=highest), None

    update, _ = lax.scan(add_subtree, jnp.zeros((NA, NA), jnp.float32), (lower_flat, upper_panels, given_inverse, kept_rows))
    ancestor = ancestor_entries - update
    top_block = ancestor[:PW, :]
    pivot = top_block[:, :PW]
    identity = jnp.eye(PW, dtype=jnp.float32)
    inverse = identity / 16.0
    for sweep in range(NEWTON):
        product = jnp.dot(pivot, inverse, precision=highest)
        inverse = jnp.dot(inverse, 2.0 * identity - product, precision=highest)
    column_factor = jnp.dot(ancestor[:, :PW], inverse, precision=highest)
    trailing = ancestor - jnp.dot(column_factor, top_block, precision=highest)
    return column_factor, trailing
```

```python
import jax
import jax.numpy as jnp
from jax import lax
from jax.sharding import PartitionSpec as P

PW = 512
NEWTON = 2
CHUNK = 512


def from_root(array, axis, root):
    mine = lax.axis_index(axis) == root
    return lax.psum(jnp.where(mine, array, jnp.zeros_like(array)), axis)


def newton(pivot):
    highest = lax.Precision.HIGHEST
    identity = jnp.eye(PW, dtype=jnp.float32)
    inverse = identity / 16.0
    for sweep in range(NEWTON):
        product = jnp.dot(pivot, inverse, precision=highest)
        inverse = jnp.dot(inverse, 2.0 * identity - product, precision=highest)
    return inverse


def generic(lower_panels, upper_panels, given_inverse, structure, ancestor_entries):
    highest = lax.Precision.HIGHEST
    subtree_count = lower_panels.shape[0]
    depth_count = lax.axis_size("depth")
    rows_count = lax.axis_size("rows")
    block_rows = lower_panels.shape[2]
    local_cols = upper_panels.shape[2]
    row_share = block_rows // rows_count
    block_count = structure.shape[1]
    block_size = depth_count * block_rows // block_count
    kept_blocks = (structure != 0).astype(jnp.bfloat16)
    lower_masked = (
        lower_panels.reshape(subtree_count, block_count, block_size, lower_panels.shape[3])
        * kept_blocks[:, :, None, None]
    ).reshape(lower_panels.shape)
    col_blocks = local_cols // block_size
    col_kept = lax.dynamic_slice_in_dim(
        kept_blocks, lax.axis_index("cols") * col_blocks, col_blocks, 1
    )
    upper_masked = (
        upper_panels.reshape(subtree_count, upper_panels.shape[1], col_blocks, block_size)
        * col_kept[:, None, :, None]
    ).reshape(upper_panels.shape)
    upper_full = lax.all_gather(upper_masked, "rows", axis=1, tiled=True)
    applied_half = jnp.einsum(
        "sik,skc->sic", given_inverse, upper_full, preferred_element_type=jnp.float32
    ).astype(jnp.bfloat16)
    update = jnp.einsum(
        "sjqk,skc->jqc",
        lax.all_gather(lower_masked, "cols", axis=3, tiled=True),
        applied_half,
        preferred_element_type=jnp.float32,
    )
    negated = (-update).reshape(depth_count * rows_count, row_share, local_cols)
    owned_sum = lax.psum_scatter(negated, ("depth", "rows"), scatter_dimension=0, tiled=True)[0]
    ancestor = ancestor_entries + owned_sum
    first_row = lax.axis_index(("depth", "rows")) * row_share
    row_offset = jnp.arange(PW, dtype=jnp.int32) - first_row
    inside = (row_offset >= 0) & (row_offset < row_share)
    picked = jnp.take(ancestor, jnp.clip(row_offset, 0, row_share - 1), axis=0)
    picked = jnp.where(inside[:, None], picked, jnp.zeros_like(picked))
    top_block = lax.psum(picked, ("depth", "rows"))
    column_panel, pivot = (
        from_root(ancestor[:, :PW], "cols", 0),
        from_root(top_block[:, :PW], "cols", 0),
    )
    inverse = newton(pivot)
    column_factor = jnp.dot(column_panel, inverse, precision=highest)
    trailing = ancestor - jnp.dot(column_factor, top_block, precision=highest)
    return (column_factor, trailing)


SWAP = [(0, 1), (1, 0)]
TURNS = ((3, 2, 1, 0), (0, 3, 2, 1), (3, 0, 1, 2), (0, 1, 2, 3))


def square_send(first, second, column):
    by_x = lax.ppermute(first, "cols", [(0, 1)])
    by_y = lax.ppermute(second, "cols", [(0, 2)])
    first = jnp.where(column == 0, first, by_x)
    second = jnp.where(column == 0, second, by_y)
    first_far = lax.ppermute(first, "cols", [(0, 2), (1, 3)])
    second_far = lax.ppermute(second, "cols", [(0, 1), (2, 3)])
    first = jnp.where(column < 2, first, first_far)
    second = jnp.where(column % 2 == 0, second, second_far)
    return first, second


def chained(lower_panels, upper_panels, given_inverse, structure, ancestor_entries):
    highest = lax.Precision.HIGHEST
    f32, f16, bf16 = jnp.float32, jnp.float16, jnp.bfloat16
    subtrees, depth_count, block_rows, depth_k = lower_panels.shape
    half_k = upper_panels.shape[1]
    local_cols = upper_panels.shape[2]
    row_share = block_rows // 2
    block_count = structure.shape[1]
    block_size = depth_count * block_rows // block_count
    z, r, c = lax.axis_index("depth"), lax.axis_index("rows"), lax.axis_index("cols")
    kept = (structure != 0).astype(bf16)

    upper_other = lax.ppermute(upper_panels, "rows", SWAP)
    ginv_own = lax.dynamic_slice_in_dim(given_inverse, r * half_k, half_k, 2)
    ginv_other = lax.dynamic_slice_in_dim(given_inverse, (1 - r) * half_k, half_k, 2)
    col_blocks = local_cols // block_size
    col_kept = lax.dynamic_slice_in_dim(kept, c * col_blocks, col_blocks, 1)
    col_kept = jnp.repeat(col_kept.astype(f32), block_size, axis=1)
    chunks = local_cols // CHUNK
    spans = [slice(j * CHUNK, (j + 1) * CHUNK) for j in range(chunks)]
    applied = []
    for span in spans:
        half = jnp.einsum(
            "sik,skc->sic", ginv_own, upper_panels[:, :, span], preferred_element_type=f32
        ) + jnp.einsum(
            "sik,skc->sic", ginv_other, upper_other[:, :, span], preferred_element_type=f32
        )
        half = (half * col_kept[:, None, span]).astype(bf16)
        applied.append(jnp.stack([half, lax.ppermute(half, "rows", SWAP)]))

    row_blocks = block_rows // block_size
    turns = jnp.array(TURNS, jnp.int32)[z]
    lower = []
    for turn in range(depth_count):
        block = turns[turn]
        rows_kept = lax.dynamic_slice_in_dim(kept, block * row_blocks, row_blocks, 1)
        picked = lax.dynamic_index_in_dim(lower_panels, block, 1, keepdims=False)
        picked = picked.reshape(subtrees, row_blocks, block_size, depth_k)
        picked = picked * rows_kept[:, :, None, None]
        picked = picked.reshape(subtrees, 2, row_share, depth_k)
        mine = lax.dynamic_index_in_dim(picked, r, 1, keepdims=False)
        theirs = lax.dynamic_index_in_dim(picked, 1 - r, 1, keepdims=False)
        both = jnp.stack([mine, lax.ppermute(theirs, "rows", SWAP)])
        lower.append(lax.all_gather(both, "cols", axis=3, tiled=True))

    def part(turn, j):
        return jnp.einsum(
            "osqk,oskc->qc", lower[turn], applied[j], preferred_element_type=f32
        )

    def along(array, pairs):
        return lax.ppermute(array, "depth", pairs)

    outer, inner, ends = [(0, 1), (3, 2)], [(1, 2), (2, 1)], [(1, 0), (2, 3)]
    ancestor = []
    for j in range(chunks):
        held = part(0, j)
        sent = along(held.astype(f16), outer)
        second = (part(1, j) + sent.astype(f32)).astype(f16)
        main, extra = along(second, outer), along(second, inner)
        third = (part(2, j) + main.astype(f32)).astype(f16)
        last = (held + extra.astype(f32)).astype(f16)
        total = (
            part(3, j)
            + along(last, ends).astype(f32)
            + along(third, outer).astype(f32)
            + along(third, inner).astype(f32)
        )
        ancestor.append(ancestor_entries[:, spans[j]] - total)

    half_rows = PW // 2
    top, top_half = [], []
    for j in range(chunks):
        block = ancestor[j][:PW]
        block = jnp.where(r == 0, block, lax.ppermute(block, "rows", [(0, 1)]))
        piece = lax.dynamic_slice_in_dim(block, r * half_rows, half_rows, 0)
        for hop in range(depth_count - 1):
            got = along(piece, [(hop, hop + 1)])
            piece = jnp.where(z == hop + 1, got, piece)
        other = lax.ppermute(piece, "rows", SWAP)
        top_half.append(piece)
        top.append(
            jnp.concatenate([jnp.where(r == 0, piece, other), jnp.where(r == 0, other, piece)])
        )

    quarter = half_rows // 2
    first, second = square_send(top_half[0][:quarter], top_half[0][quarter:], c)
    piece = jnp.concatenate([first, second])
    other = lax.ppermute(piece, "rows", SWAP)
    pivot = jnp.concatenate([jnp.where(r == 0, piece, other), jnp.where(r == 0, other, piece)])
    first, second = square_send(
        ancestor[0][: row_share // 2], ancestor[0][row_share // 2 :], c
    )
    column_panel = jnp.concatenate([first, second])
    inverse = newton(pivot)
    column_factor = jnp.dot(column_panel, inverse, precision=highest)
    trailing = jnp.concatenate(
        [
            ancestor[j] - jnp.dot(column_factor, top[j], precision=highest)
            for j in range(chunks)
        ],
        axis=1,
    )
    return (column_factor, trailing)


def local(*args):
    lower_panels, upper_panels = args[0], args[1]
    square = lax.axis_size("depth") == 4 and lax.axis_size("cols") == 4
    pairs = lax.axis_size("rows") == 2
    if square and pairs and PW == CHUNK:
        if lower_panels.shape[2] // 2 >= PW and upper_panels.shape[2] % CHUNK == 0:
            return chained(*args)
    return generic(*args)


def solution(mesh):
    return jax.shard_map(
        local,
        mesh=mesh,
        in_specs=(
            P("depth", None, None, ("rows", "cols")),
            P("depth", "rows", "cols"),
            P("depth", "rows", None),
            P("depth", None),
            P(("depth", "rows"), "cols"),
        ),
        out_specs=(P(("depth", "rows"), None), P(("depth", "rows"), "cols")),
        check_vma=False,
    )
```

```python
import jax
import jax.numpy as jnp
from jax import lax
from jax.sharding import PartitionSpec as P

PW = 512
NEWTON = 2
CHUNK = 512


def from_root(array, axis, root):
    mine = lax.axis_index(axis) == root
    return lax.psum(jnp.where(mine, array, jnp.zeros_like(array)), axis)


def newton(pivot):
    highest = lax.Precision.HIGHEST
    identity = jnp.eye(PW, dtype=jnp.float32)
    inverse = identity / 16.0
    for _ in range(NEWTON):
        product = jnp.dot(pivot, inverse, precision=highest)
        inverse = jnp.dot(inverse, 2.0 * identity - product, precision=highest)
    return inverse


def generic(lower_panels, upper_panels, given_inverse, structure, ancestor_entries):
    highest = lax.Precision.HIGHEST
    subtree_count = lower_panels.shape[0]
    depth_count = lax.axis_size("depth")
    rows_count = lax.axis_size("rows")
    block_rows = lower_panels.shape[2]
    local_cols = upper_panels.shape[2]
    row_share = block_rows // rows_count
    block_count = structure.shape[1]
    block_size = depth_count * block_rows // block_count
    kept_blocks = (structure != 0).astype(jnp.bfloat16)
    lower_masked = (
        lower_panels.reshape(subtree_count, block_count, block_size, lower_panels.shape[3])
        * kept_blocks[:, :, None, None]
    ).reshape(lower_panels.shape)
    col_blocks = local_cols // block_size
    col_kept = lax.dynamic_slice_in_dim(
        kept_blocks, lax.axis_index("cols") * col_blocks, col_blocks, 1
    )
    upper_masked = (
        upper_panels.reshape(subtree_count, upper_panels.shape[1], col_blocks, block_size)
        * col_kept[:, None, :, None]
    ).reshape(upper_panels.shape)
    upper_full = lax.all_gather(upper_masked, "rows", axis=1, tiled=True)
    applied_half = jnp.einsum(
        "sik,skc->sic", given_inverse, upper_full, preferred_element_type=jnp.float32
    ).astype(jnp.bfloat16)
    update = jnp.einsum(
        "sjqk,skc->jqc",
        lax.all_gather(lower_masked, "cols", axis=3, tiled=True),
        applied_half,
        preferred_element_type=jnp.float32,
    )
    negated = (-update).reshape(depth_count * rows_count, row_share, local_cols)
    owned_sum = lax.psum_scatter(negated, ("depth", "rows"), scatter_dimension=0, tiled=True)[0]
    ancestor = ancestor_entries + owned_sum
    first_row = lax.axis_index(("depth", "rows")) * row_share
    row_offset = jnp.arange(PW, dtype=jnp.int32) - first_row
    inside = (row_offset >= 0) & (row_offset < row_share)
    picked = jnp.take(ancestor, jnp.clip(row_offset, 0, row_share - 1), axis=0)
    picked = jnp.where(inside[:, None], picked, jnp.zeros_like(picked))
    top_block = lax.psum(picked, ("depth", "rows"))
    column_panel, pivot = (
        from_root(ancestor[:, :PW], "cols", 0),
        from_root(top_block[:, :PW], "cols", 0),
    )
    inverse = newton(pivot)
    column_factor = jnp.dot(column_panel, inverse, precision=highest)
    trailing = ancestor - jnp.dot(column_factor, top_block, precision=highest)
    return (column_factor, trailing)


SWAP = [(0, 1), (1, 0)]
SWAP_X = [(0, 1), (1, 0), (2, 3), (3, 2)]
SWAP_Y = [(0, 2), (2, 0), (1, 3), (3, 1)]
OUTER, INNER, ENDS = [(0, 1), (3, 2)], [(1, 2), (2, 1)], [(1, 0), (2, 3)]
TURNS = ((3, 2, 1, 0), (0, 3, 2, 1), (3, 0, 1, 2), (0, 1, 2, 3))


def square_send(first, second, column):
    by_x = lax.ppermute(first, "cols", [(0, 1)])
    by_y = lax.ppermute(second, "cols", [(0, 2)])
    first = jnp.where(column == 0, first, by_x)
    second = jnp.where(column == 0, second, by_y)
    first_far = lax.ppermute(first, "cols", [(0, 2), (1, 3)])
    second_far = lax.ppermute(second, "cols", [(0, 1), (2, 3)])
    first = jnp.where(column < 2, first, first_far)
    second = jnp.where(column % 2 == 0, second, second_far)
    return first, second


def square_gather(own):
    by_x = lax.ppermute(own, "cols", SWAP_X)
    by_y = lax.ppermute(own, "cols", SWAP_Y)
    far = jnp.stack([lax.ppermute(by_y[0], "cols", SWAP_X), lax.ppermute(by_x[1], "cols", SWAP_Y)])
    return jnp.concatenate([own, by_x, by_y, far], axis=own.ndim - 1)


def chained(lower_panels, upper_panels, given_inverse, structure, ancestor_entries):
    high = lax.Precision.HIGH
    f32, f16, bf16 = jnp.float32, jnp.float16, jnp.bfloat16
    subtrees, depth_count, block_rows, depth_k = lower_panels.shape
    half_k = upper_panels.shape[1]
    local_cols = upper_panels.shape[2]
    row_share = block_rows // 2
    block_count = structure.shape[1]
    block_size = depth_count * block_rows // block_count
    z, r, c = lax.axis_index("depth"), lax.axis_index("rows"), lax.axis_index("cols")
    kept = (structure != 0).astype(bf16)

    row_blocks = block_rows // block_size

    def masked_rows(block, half):
        half_blocks = row_blocks // 2
        rows_kept = lax.dynamic_slice_in_dim(
            kept, block * row_blocks + half * half_blocks, half_blocks, 1
        )
        picked = lax.dynamic_slice(
            lower_panels,
            (0, block, half * row_share, 0),
            (subtrees, 1, row_share, depth_k),
        )
        picked = picked.reshape(subtrees, half_blocks, block_size, depth_k)
        picked = picked * rows_kept[:, :, None, None]
        return picked.reshape(subtrees, row_share, depth_k)

    def masked_block(turn):
        block = sum(jnp.where(z == at, TURNS[at][turn], 0) for at in range(depth_count))
        return masked_rows(block, r), masked_rows(block, 1 - r)

    mine, theirs = zip(*[masked_block(turn) for turn in range(depth_count)])
    first_got = lax.ppermute(theirs[0], "rows", SWAP)
    upper_other = lax.ppermute(upper_panels, "rows", SWAP)
    later_got = lax.ppermute(jnp.stack(theirs[1:]), "rows", SWAP)
    got = [first_got] + [later_got[turn] for turn in range(depth_count - 1)]
    lower = [square_gather(jnp.stack([mine[turn], got[turn]])) for turn in range(depth_count)]

    def ginv_half(half):
        return jnp.concatenate(
            [
                lax.dynamic_slice(
                    given_inverse,
                    (0, (c ^ near) * depth_k, half * half_k),
                    (subtrees, depth_k, half_k),
                )
                for near in range(4)
            ],
            axis=1,
        )

    ginv_own, ginv_other = ginv_half(r), ginv_half(1 - r)
    col_blocks = local_cols // block_size
    col_kept = lax.dynamic_slice_in_dim(kept, c * col_blocks, col_blocks, 1)
    col_kept = jnp.repeat(col_kept.astype(f32), block_size, axis=1)
    chunks = local_cols // CHUNK
    spans = [slice(j * CHUNK, (j + 1) * CHUNK) for j in range(chunks)]
    applied = []
    for span in spans:
        half = jnp.einsum(
            "sik,skc->sic", ginv_own, upper_panels[:, :, span], preferred_element_type=f32
        ) + jnp.einsum(
            "sik,skc->sic", ginv_other, upper_other[:, :, span], preferred_element_type=f32
        )
        half = (half * col_kept[:, None, span]).astype(bf16)
        applied.append(jnp.stack([half, lax.ppermute(half, "rows", SWAP)]))

    def part(turn, j):
        return jnp.einsum(
            "osqk,oskc->qc", lower[turn], applied[j], preferred_element_type=f32
        )

    base, ancestor = [], []
    for j in range(chunks):
        held = part(0, j)
        sent = lax.ppermute(held.astype(f16), "depth", OUTER)
        second = (part(1, j) + sent.astype(f32)).astype(f16)
        main = lax.ppermute(second, "depth", OUTER)
        extra = lax.ppermute(second, "depth", INNER)
        third = (part(2, j) + main.astype(f32)).astype(f16)
        last = (held + extra.astype(f32)).astype(f16)
        far = lax.ppermute(last, "depth", ENDS)
        base.append(ancestor_entries[:, spans[j]] - part(3, j) - far.astype(f32))
        near = lax.ppermute(third, "depth", OUTER).astype(f32)
        near = near + lax.ppermute(third, "depth", INNER).astype(f32)
        ancestor.append(base[j] - near)

    half_rows = PW // 2

    def up_depth(block):
        below = lax.ppermute(block, "rows", [(0, 1)])
        block = jnp.where(r == 0, block, below)
        piece = lax.dynamic_slice_in_dim(block, r * half_rows, half_rows, 0)
        for hop in range(depth_count - 1):
            got = lax.ppermute(piece, "depth", [(hop, hop + 1)])
            piece = jnp.where(z == hop + 1, got, piece)
        return piece

    def both_halves(piece):
        other = lax.ppermute(piece, "rows", SWAP)
        return jnp.concatenate(
            [jnp.where(r == 0, piece, other), jnp.where(r == 0, other, piece)]
        )

    pivot_half = up_depth(base[0][:PW])
    top_rest = jnp.concatenate([part_of[:PW].astype(f16) for part_of in base[1:]], axis=1)
    top = jnp.concatenate(
        [both_halves(pivot_half), both_halves(up_depth(top_rest)).astype(f32)],
        axis=1,
    )
    quarter = half_rows // 2
    pivot = both_halves(jnp.concatenate(square_send(pivot_half[:quarter], pivot_half[quarter:], c)))
    column_panel = jnp.concatenate(
        square_send(ancestor[0][: row_share // 2], ancestor[0][row_share // 2 :], c)
    )
    column_factor = jnp.dot(column_panel, newton(pivot), precision=high)
    trailing = jnp.concatenate(
        [
            ancestor[j] - jnp.dot(column_factor, top[:, spans[j]], precision=high)
            for j in range(chunks)
        ],
        axis=1,
    )
    return (column_factor, trailing)


def chained_fits(mesh):
    return mesh.shape["depth"] == 4 and mesh.shape["cols"] == 4 and mesh.shape["rows"] == 2


def local(*args):
    return chained(*args)


def solution(mesh):
    body = local if chained_fits(mesh) else generic
    step = jax.shard_map(
        body,
        mesh=mesh,
        in_specs=(
            P("depth", None, None, ("rows", "cols")),
            P("depth", "rows", "cols"),
            P("depth", "rows", None),
            P("depth", None),
            P(("depth", "rows"), "cols"),
        ),
        out_specs=(P(("depth", "rows"), None), P(("depth", "rows"), "cols")),
        check_vma=False,
    )
    if body is generic:
        return step
    return step
```
